32 devices in a mesh: grp: 4 (over y, core), tp: 8 (over z, x).
Axes of the slice: x: 2, y: 2, z: 4, core: 2. Of those that a mesh axis runs over, the one named last changes fastest.
Arguments:
- tokens: bfloat16 [64, 256, 1152], P(('grp', 'tp')), may hold values from -4 to 4
- cond: bfloat16 [64, 1152], P('grp'), may hold values from -2 to 2
- keep_counts: int32 [64], P('grp'), may hold values from 64 to 192, as said below
- orders: int32 [64, 256], P('grp'), may hold values from 0 to 255, each once within a row
- ada_weight: bfloat16 [1152, 6, 1152], P(None, None, 'tp'), may hold values from -0.1875 to 0.1875
- ada_bias: bfloat16 [6, 1152], P(None, 'tp'), may hold values from -0.3984375 to 0.3984375
- qkv_weight: bfloat16 [1152, 3, 1152], P(None, None, 'tp'), may hold values from -0.1875 to 0.1875
- qv_bias: bfloat16 [2, 1152], P(None, 'tp'), may hold values from -0.3984375 to 0.3984375
- out_weight: bfloat16 [1152, 1152], P('tp'), may hold values from -0.75 to 0.75
- out_bias: bfloat16 [1152], replicated, may hold values from -0.3984375 to 0.3984375
- fc1_weight: bfloat16 [1152, 4608], P(None, 'tp'), may hold values from -0.1875 to 0.1875
- fc1_bias: bfloat16 [4608], P('tp'), may hold values from -0.3984375 to 0.3984375
- fc2_weight: bfloat16 [4608, 1152], P('tp'), may hold values from -0.09375 to 0.09375
- fc2_bias: bfloat16 [1152], replicated, may hold values from -0.3984375 to 0.3984375
- cotangent: bfloat16 [64, 256, 1152], P(('grp', 'tp')), may hold values from -4 to 4
Outputs:
- block_out: float32 [64, 256, 1152], P(('grp', 'tp'))
- tokens_grad: float32 [64, 256, 1152], P(('grp', 'tp'))
- cond_grad: float32 [64, 1152], P('grp', 'tp')
- ada_weight_grad: float32 [1152, 6, 1152], P(None, None, 'tp')
- ada_bias_grad: float32 [6, 1152], P(None, 'tp')
- qkv_weight_grad: float32 [1152, 3, 1152], P(None, None, 'tp')
- qv_bias_grad: float32 [2, 1152], P(None, 'tp')
- out_weight_grad: float32 [1152, 1152], P('tp')
- out_bias_grad: float32 [1152], P('tp')
- fc1_weight_grad: float32 [1152, 4608], P(None, 'tp')
- fc1_bias_grad: float32 [4608], P('tp')
- fc2_weight_grad: float32 [4608, 1152], P('tp')
- fc2_bias_grad: float32 [1152], P('tp')
- token_counts: int32 [2], replicated
The draws below stay inside these ranges and needn't reach their ends.
Inputs may be any that keep to these rules, and one draw needn't show every extreme that they name: `keep_counts`: the images of a group keep counts near a common level, which rises from the first group to the last. `orders`: each row holds every number of 0 to 255 once.
All inputs are finite; a program needn't handle non-finite values.
Results may differ from the reference program's by a relative error of at most 0.02.
Values may be sent and summed in bfloat16 or wider, within the bound.
A program may use at most 320 MiB of HBM per device.

```python
import jax
import jax.numpy as jnp
from jax import lax

D = 1152
HEADS = 16
HEAD_DIM = 72
FF = 4608
TOK_IMG = 256
IMG_GRP = 16
IMAGES = 64


def draw_keep_counts(key, part):
    low_end = TOK_IMG // 4
    high_end = 3 * TOK_IMG // 4
    groups = IMAGES // IMG_GRP
    image_ids = jnp.arange(IMAGES, dtype=jnp.int32)
    group_of = image_ids // IMG_GRP
    base_count = low_end + (high_end - low_end) * group_of // max(groups - 1, 1)
    jitter = jax.random.randint(key, (IMAGES,), -(TOK_IMG // 16), TOK_IMG // 16 + 1, dtype=jnp.int32)
    counts = jnp.clip(base_count + jitter, low_end, high_end)
    counts = counts.at[0].set(low_end).at[IMAGES - 1].set(high_end)
    return counts.astype(jnp.int32)


def level_of(key, dims, shards, low, top_value):
    loudness = 1.0
    for dim, parts in shards:
        draws = jax.random.uniform(jax.random.fold_in(jax.random.fold_in(key, 6), dim), (parts,), jnp.float32, low / len(shards), top_value / len(shards))
        loudness = loudness * jnp.repeat(jnp.exp(draws), dims[dim] // parts).reshape((-1,) + (1,) * (len(dims) - 1 - dim))
    return loudness


def bell_draw(stream_key, extent, width, most, cuts=(), kind=jnp.bfloat16):
    array = jax.random.normal(stream_key, extent, jnp.float32) * width
    if len(cuts) > 0:
        array = level_of(stream_key, extent, cuts, -0.22, 0.18) * array
    return jnp.clip(array, min=-most, max=most).astype(kind)


def setup_inputs(seed: int = 0) -> dict:
    key_list = jax.random.split(jax.random.key(seed), 16)
    return {
        "tokens": bell_draw(key_list[0], (IMAGES, TOK_IMG, D), 1.0, 4.0, ((0, 32),)),
        "cond": jnp.clip(jax.random.uniform(key_list[1], (IMAGES, D), jnp.float32, -2.0, 2.0) * level_of(key_list[1], (IMAGES, D), ((0, 4),), -0.4, 0.0), -2.0, 2.0).astype(jnp.bfloat16),
        "keep_counts": draw_keep_counts(jax.random.fold_in(key_list[15], 71), 0),
        "orders": jax.vmap(lambda own: jax.random.permutation(own, TOK_IMG))(jax.random.split(key_list[3], IMAGES)).reshape((IMAGES, TOK_IMG)).astype(jnp.int32),
        "ada_weight": bell_draw(key_list[4], (D, 6, D), D ** -0.5, 0.1875, ((2, 8),)),
        "ada_bias": jnp.clip(jax.random.uniform(key_list[5], (6, D), jnp.float32, -0.3984375, 0.3984375) * level_of(key_list[5], (6, D), ((1, 8),), -0.4, 0.0), -0.3984375, 0.3984375).astype(jnp.bfloat16),
        "qkv_weight": bell_draw(key_list[6], (D, 3, D), D ** -0.5, 0.1875, ((2, 8),)),
        "qv_bias": jnp.clip(jax.random.uniform(key_list[7], (2, D), jnp.float32, -0.3984375, 0.3984375) * level_of(key_list[7], (2, D), ((1, 8),), -0.4, 0.0), -0.3984375, 0.3984375).astype(jnp.bfloat16),
        "out_weight": bell_draw(key_list[8], (D, D), (D // 16) ** -0.5, 0.75, ((0, 8),)),
        "out_bias": jnp.clip(jax.random.uniform(key_list[9], (D,), jnp.float32, -0.3984375, 0.3984375), -0.3984375, 0.3984375).astype(jnp.bfloat16),
        "fc1_weight": bell_draw(key_list[10], (D, FF), D ** -0.5, 0.1875, ((1, 8),)),
        "fc1_bias": jnp.clip(jax.random.uniform(key_list[11], (FF,), jnp.float32, -0.3984375, 0.3984375) * level_of(key_list[11], (FF,), ((0, 8),), -0.4, 0.0), -0.3984375, 0.3984375).astype(jnp.bfloat16),
        "fc2_weight": bell_draw(key_list[12], (FF, D), FF ** -0.5, 0.09375, ((0, 8),)),
        "fc2_bias": jnp.clip(jax.random.uniform(key_list[13], (D,), jnp.float32, -0.3984375, 0.3984375), -0.3984375, 0.3984375).astype(jnp.bfloat16),
        "cotangent": bell_draw(key_list[14], (IMAGES, TOK_IMG, D), 1.0, 4.0, ((0, 32),)),
    }


@jax.custom_vjp
def low(v):
    return lax.optimization_barrier(v.astype(jnp.bfloat16)).astype(jnp.float32)

@jax.custom_vjp
def low_back(v):
    return v

def low_keep(v):
    return (low(v), None)

def low_pass(kept, grad):
    return (grad,)

def back_keep(v):
    return (v, None)

def back_low(kept, grad):
    return (low(grad),)
low.defvjp(low_keep, low_pass)
low_back.defvjp(back_keep, back_low)

def product_of(form, left, right):
    return jnp.einsum(form, left, right, precision=lax.Precision.HIGHEST)

def layer_norm(values):
    centred = values - lax.optimization_barrier(jnp.mean(values, axis=-1, keepdims=True))
    return centred * lax.rsqrt(lax.optimization_barrier(jnp.mean(centred * centred, axis=-1, keepdims=True)) + 1e-06)

def kept_mask(counts_in, orders_in):
    tok_count = orders_in.shape[1]
    places = lax.broadcasted_iota(jnp.int32, (1, 1, tok_count), 2)
    slot_ids = lax.broadcasted_iota(jnp.int32, (1, tok_count, 1), 1)
    position = lax.optimization_barrier(jnp.sum(jnp.where(orders_in[:, :, None] == places, slot_ids, 0), axis=1)).astype(jnp.int32)
    return (position < counts_in.astype(jnp.int32)[:, None]).astype(jnp.float32)

def group_forward(params, resid_rows, cond_rows, keep_rows):
    ada_weight, ada_bias, qkv_weight, qv_bias, out_weight, out_bias, fc1_weight, fc1_bias, fc2_weight, fc2_bias = params
    images = resid_rows.shape[0]
    silu_cond = low(jax.nn.silu(cond_rows))
    modulation = low_back(product_of('id,dke->ike', silu_cond, ada_weight) + ada_bias[None])
    shift_one = modulation[:, 0][:, None, :]
    scale_one = modulation[:, 1][:, None, :]
    gate_one = modulation[:, 2][:, None, :]
    shift_two = modulation[:, 3][:, None, :]
    scale_two = modulation[:, 4][:, None, :]
    gate_two = modulation[:, 5][:, None, :]
    attn_in = low(layer_norm(resid_rows) * (1.0 + scale_one) + shift_one)
    bias_all = jnp.stack([qv_bias[0], jnp.zeros_like(qv_bias[0]), qv_bias[1]])
    projected = low_back(low(product_of('itd,dke->itke', attn_in, qkv_weight) + bias_all))
    qkv_parts = projected.reshape(images, TOK_IMG, 3, HEADS, HEAD_DIM)
    scores = product_of('iqhe,ikhe->ihqk', qkv_parts[:, :, 0], qkv_parts[:, :, 1]) * HEAD_DIM ** (-0.5)
    scores = low_back(scores)
    scores = jnp.where(keep_rows[:, None, None, :] > 0.5, scores, -1e+30)
    attn_probs = low(jax.nn.softmax(scores, axis=-1))
    attn_out = product_of('ihqk,ikhe->iqhe', attn_probs, qkv_parts[:, :, 2]).reshape(images, TOK_IMG, D)
    attn_out = low_back(low(attn_out))
    branch_one = low_back(product_of('ite,ed->itd', attn_out, out_weight) + out_bias)
    keep_col = keep_rows[:, :, None]
    hidden_res = resid_rows + keep_col * gate_one * branch_one
    mlp_in = low(layer_norm(hidden_res) * (1.0 + scale_two) + shift_two)
    pre_act = low_back(product_of('itd,df->itf', mlp_in, fc1_weight) + fc1_bias)
    activated = low(jax.nn.gelu(pre_act, approximate=True))
    branch_two = low_back(product_of('itf,fd->itd', activated, fc2_weight) + fc2_bias)
    return hidden_res + keep_col * gate_two * branch_two

def reference(tokens, cond, keep_counts, orders, ada_weight, ada_bias, qkv_weight, qv_bias, out_weight, out_bias, fc1_weight, fc1_bias, fc2_weight, fc2_bias, cotangent):
    groups = IMAGES // IMG_GRP
    keep_all = kept_mask(keep_counts, orders).reshape(groups, IMG_GRP, TOK_IMG)
    params = tuple((array_item.astype(jnp.float32) for array_item in (ada_weight, ada_bias, qkv_weight, qv_bias, out_weight, out_bias, fc1_weight, fc1_bias, fc2_weight, fc2_bias)))
    resid_all = tokens.astype(jnp.float32).reshape(groups, IMG_GRP, TOK_IMG, D)
    cond_all = cond.astype(jnp.float32).reshape(groups, IMG_GRP, D)
    step_fn = jax.checkpoint(group_forward)

    def forward(params_in, resid_in, cond_in):

        def scan_step(carried, inputs):
            return (carried, step_fn(params_in, inputs[0], inputs[1], inputs[2]))
        return lax.scan(scan_step, jnp.zeros((), jnp.float32), (resid_in, cond_in, keep_all))[1]
    block_out, pullback = jax.vjp(forward, params, resid_all, cond_all)
    param_grads, tokens_grad, cond_grad = pullback(cotangent.astype(jnp.float32).reshape(groups, IMG_GRP, TOK_IMG, D))
    kept_int = jnp.sum(keep_counts).astype(jnp.int32)
    kept_total = kept_int.astype(jnp.float32)
    scaled = tuple((array_item / kept_total for array_item in param_grads))
    token_counts = jnp.stack([kept_int, IMAGES * TOK_IMG - kept_int]).astype(jnp.int32)
    return (block_out.reshape(IMAGES, TOK_IMG, D), tokens_grad.reshape(IMAGES, TOK_IMG, D), cond_grad.reshape(IMAGES, D), scaled[0], scaled[1], scaled[2], scaled[3], scaled[4], scaled[5], scaled[6], scaled[7], scaled[8], scaled[9], token_counts)
```

```python
import functools

import jax
import jax.numpy as jnp
from jax import lax
from jax.experimental import pallas as pl
from jax.experimental.pallas import tpu as pltpu
from jax.sharding import PartitionSpec as P

HEAD_DIM = 72
SCALE = HEAD_DIM ** (-0.5)
F32 = jnp.float32
BF16 = jnp.bfloat16
NT = (((1,), (1,)), ((), ()))
NN = (((1,), (0,)), ((), ()))
TN = (((0,), (0,)), ((), ()))


def dot(a, b, dims):
    return lax.dot_general(a, b, dims, preferred_element_type=F32)


MESH = pl.DeviceIdType.MESH


class Links:
    def __init__(self, tp_count, grp_count):
        self.tp_count = tp_count
        self.cores = 2 if grp_count % 2 == 0 else 1
        self.outer = grp_count // self.cores
        self.steps = (tp_count - 1) // 2
        self.tp = lax.axis_index("tp")
        self.grp = lax.axis_index("grp")
        self.core = self.grp % self.cores
        half = (tp_count + 1) // 2
        self.half = half
        tp = self.tp
        self.place = jnp.where(tp % 2 == 0, tp // 2, half + (tp_count - 1 - tp) // 2)

    def shard(self, distance):
        ring = (self.place + distance + self.tp_count) % self.tp_count
        return jnp.where(ring < self.half, 2 * ring, 2 * (self.tp_count - 1 - ring) + 1)

    def up(self):
        return (self.grp, self.shard(1))

    def down(self):
        return (self.grp, self.shard(-1))

    def sibling(self):
        return (self.grp + 1 - 2 * self.core, self.tp)

    def across(self):
        return ((self.grp + self.cores) % (self.cores * self.outer), self.tp)

    def greet(self, use_core, use_outer, split=True):
        peers = [self.up(), self.down()]
        if use_core:
            peers.append(self.sibling())
        if use_outer and split:
            peers.append(self.across())
        barrier = pltpu.get_barrier_semaphore()
        for peer in peers:
            pl.semaphore_signal(barrier, inc=1, device_id=peer, device_id_type=MESH)
        pl.semaphore_wait(barrier, len(peers))


class Way:
    def __init__(self, tp_count, grp_count, use_core, use_outer, splits):
        self.cores = 2 if use_core else 1
        self.outers = 2 if use_outer else 1
        self.use_core, self.use_outer = use_core, use_outer
        self.shares = self.cores * self.outers
        self.splits = splits
        self.steps = (tp_count - 1) // 2
        self.distances = [0] + [s * d for d in range(1, self.steps + 1) for s in (-1, 1)]
        if tp_count % 2 == 0:
            self.distances.append(tp_count // 2)
        self.arrays = len(splits)

    def share(self, links, outer_flip=0, core_flip=0):
        share = 0
        if self.use_outer:
            share = (links.grp // links.cores + outer_flip) % 2
        if self.use_core:
            share = share * 2 + (links.core + core_flip) % 2
        return share


def remote(src, dst, sems, index, device):
    return pltpu.make_async_remote_copy(
        src_ref=src, dst_ref=dst, send_sem=sems[0].at[index], recv_sem=sems[1].at[index],
        device_id=device, device_id_type=MESH,
    )


def sem_pair(*shape):
    return [pltpu.SemaphoreType.DMA(shape), pltpu.SemaphoreType.DMA(shape)]


class Gather:
    @staticmethod
    def scratch(way):
        n, a = len(way.distances), way.arrays
        shapes = sem_pair(2, a, way.steps + 2)
        shapes += sem_pair(a, n) + sem_pair(2, a, n)
        return shapes + [pltpu.SemaphoreType.DMA((a,))]

    def __init__(self, way, links, own, full, scratch):
        self.way, self.links, self.own, self.full = way, links, own, full
        self.ring, self.outer, self.core = scratch[0:2], scratch[2:4], scratch[4:6]
        self.local = scratch[6]
        self.pending = []

    def slot(self, a, index, **flips):
        way = self.way
        return self.full[a].at[self.links.shard(way.distances[index]), way.share(self.links, **flips)]

    def hop(self, a, index, direction, step, src=None, rows=None):
        src = self.slot(a, index) if src is None else src
        dst = self.slot(a, index)
        if rows is not None:
            src, dst = src.at[rows], dst.at[rows]
        device = self.links.up() if direction == 0 else self.links.down()
        return remote(src, dst, self.ring, (direction, a, step), device)

    def spread(self, a, index, src=None):
        src = self.slot(a, index) if src is None else src
        if self.way.use_outer:
            copy = remote(src, self.slot(a, index), self.outer, (a, index), self.links.across())
            copy.start()
            self.pending.append(copy)
        if self.way.use_core:
            copy = remote(src, self.slot(a, index), self.core, (0, a, index), self.links.sibling())
            copy.start()
            self.pending.append(copy)

    def relay(self, index):
        if not self.way.use_outer:
            return
        for a in range(self.way.arrays):
            slot = self.slot(a, index, outer_flip=1)
            remote(slot, slot, self.outer, (a, index), self.links.across()).wait_recv()
            if self.way.use_core:
                copy = remote(slot, slot, self.core, (1, a, index), self.links.sibling())
                copy.start()
                self.pending.append(copy)

    def halves(self, a):
        low = self.way.splits[a]
        rows = self.own[a].shape[0]
        parts = []
        if low > 0:
            parts.append((0, pl.ds(0, low)))
        if low < rows:
            parts.append((1, pl.ds(low, rows - low)))
        return parts

    def start(self):
        for a in range(self.way.arrays):
            for direction in range(2):
                copy = self.hop(a, 0, direction, 1, src=self.own[a])
                copy.start()
                self.pending.append(copy)
        for a in range(self.way.arrays):
            self.spread(a, 0, src=self.own[a])
            copy = pltpu.make_async_copy(self.own[a], self.slot(a, 0), self.local.at[a])
            copy.start()

    def round(self, step):
        way = self.way
        if step <= way.steps:
            for a in range(way.arrays):
                for direction in range(2):
                    index = 2 * step - 1 + direction
                    self.hop(a, index, direction, step).wait_recv()
                    if step < way.steps:
                        copy = self.hop(a, index, direction, step + 1)
                        copy.start()
                        self.pending.append(copy)
                    elif len(way.distances) % 2 == 0:
                        for side, rows in self.halves(a):
                            if side == direction:
                                copy = self.hop(a, index, direction, step + 1, rows=rows)
                                copy.start()
                                self.pending.append(copy)
            for a in range(way.arrays):
                for direction in range(2):
                    self.spread(a, 2 * step - 1 + direction)
        else:
            last = len(way.distances) - 1
            for a in range(way.arrays):
                for side, rows in self.halves(a):
                    self.hop(a, last, side, step, rows=rows).wait_recv()
                self.spread(a, last)

    def rounds(self):
        return self.way.steps + (1 if len(self.way.distances) % 2 == 0 else 0)

    def tail(self):
        for index in range(max(0, 2 * self.rounds() - 3), len(self.way.distances)):
            self.relay(index)

    def finish(self):
        way = self.way
        for a in range(way.arrays):
            pltpu.make_async_copy(self.own[a], self.slot(a, 0), self.local.at[a]).wait()
        if way.use_core:
            for index in range(len(way.distances)):
                for a in range(way.arrays):
                    for o in range(way.outers):
                        slot = self.slot(a, index, outer_flip=o, core_flip=1)
                        remote(slot, slot, self.core, (o, a, index), self.links.sibling()).wait_recv()
        for copy in self.pending:
            copy.wait_send()


def gather_kernel(ways, set_sizes, tp_count, grp_count, *refs):
    links = Links(tp_count, grp_count)
    arrays = sum(way.arrays for way in ways)
    own, full, scratch = refs[:arrays], refs[arrays : 2 * arrays], refs[2 * arrays :]
    gathers, at = [], 0
    for i, way in enumerate(ways):
        gathers.append(
            Gather(way, links, own[at : at + way.arrays], full[at : at + way.arrays], scratch[7 * i : 7 * i + 7])
        )
        at += way.arrays
    links.greet(any(w.use_core for w in ways), any(w.use_outer for w in ways))
    sets, at = [], 0
    for size in set_sizes:
        sets.append(gathers[at : at + size])
        at += size
    for gather in sets[0]:
        gather.start()
    for i, group in enumerate(sets):
        rounds, steps = group[0].rounds(), group[0].way.steps
        for step in range(1, rounds + 1):
            for gather in group:
                gather.round(step)
            if step == steps and i + 1 < len(sets):
                for gather in sets[i + 1]:
                    gather.start()
            for gather in group:
                for index in [0] if step == 2 else [2 * step - 5, 2 * step - 4] if step > 2 else []:
                    gather.relay(index)
            if step == 1 and i > 0:
                for gather in sets[i - 1]:
                    gather.tail()
    for gather in sets[-1]:
        gather.tail()
    for gather in gathers:
        gather.finish()


def gather_weights(ways, set_sizes, pieces, tp_count, grp_count, collective_id):
    arrays = [x for p in pieces for x in p]
    shares = [way.shares for way in ways for _ in range(way.arrays)]
    out = pl.pallas_call(
        functools.partial(gather_kernel, ways, set_sizes, tp_count, grp_count),
        in_specs=[pl.BlockSpec(memory_space=pltpu.VMEM)] * len(arrays),
        out_specs=[pl.BlockSpec(memory_space=pltpu.HBM)] * len(arrays),
        out_shape=[
            jax.ShapeDtypeStruct((tp_count, s) + x.shape, x.dtype) for s, x in zip(shares, arrays)
        ],
        scratch_shapes=[s for way in ways for s in Gather.scratch(way)],
        compiler_params=pltpu.CompilerParams(collective_id=collective_id, has_side_effects=True),
    )(*arrays)
    return out


def sum_rows(target, terms):
    rows = target.shape[0]

    def some(span):
        total = terms[0][span, :].astype(F32)
        for term in terms[1:]:
            total = total + term[span, :].astype(F32)
        target[span, :] = total.astype(target.dtype)

    whole = rows // 16

    def step(i, carry):
        some(pl.ds(pl.multiple_of(i * 16, 16), 16))
        return carry

    lax.fori_loop(0, whole, step, 0)
    if rows % 16:
        some(pl.ds(whole * 16, rows % 16))


class Reduce:
    @staticmethod
    def scratch(way, rows, width):
        n = len(way.distances)
        shapes = []
        for a in range(way.arrays):
            shapes += [
                pltpu.VMEM((n, way.outers, rows[a], width), BF16),
                pltpu.VMEM((n if way.use_outer else 1, rows[a], width), BF16),
                pltpu.VMEM((2, way.steps + 1, rows[a], width), BF16),
                pltpu.VMEM((way.shares, rows[a], width), BF16),
                pltpu.VMEM((1, rows[a], width), BF16),
            ]
        a = way.arrays
        shapes += sem_pair(2, a, way.steps + 2) + sem_pair(a, n) + sem_pair(2, a, n)
        return shapes + sem_pair(a) + sem_pair(2, a)

    @staticmethod
    def scratch_count(way):
        return 5 * way.arrays + 10

    def __init__(self, way, links, parts, scratch):
        self.way, self.links, self.parts = way, links, parts
        bufs, sems = scratch[: 5 * way.arrays], scratch[5 * way.arrays :]
        self.acc, self.cross, self.land, self.total, self.other = (bufs[k::5] for k in range(5))
        self.ring, self.outer, self.core = sems[0:2], sems[2:4], sems[4:6]
        self.last_outer, self.last_core = sems[6:8], sems[8:10]
        self.pending = []

    def part(self, a, index, **flips):
        way = self.way
        return self.parts[a].at[self.links.shard(way.distances[index]), way.share(self.links, **flips)]

    def send(self, src, dst, sems, index, device):
        copy = remote(src, dst, sems, index, device)
        copy.start()
        self.pending.append(copy)

    def order(self):
        return list(range(len(self.way.distances)))[::-1]

    def swap(self, index):
        way = self.way
        if way.use_core:
            for o in range(way.outers)[::-1]:
                for a in range(way.arrays):
                    self.send(
                        self.part(a, index, outer_flip=o, core_flip=1),
                        self.acc[a].at[index, o], self.core, (o, a, index), self.links.sibling(),
                    )

    def wait_swap(self, a, index, o):
        if self.way.use_core:
            slot = self.acc[a].at[index, o]
            remote(slot, slot, self.core, (o, a, index), self.links.sibling()).wait_recv()

    def crossing(self, index):
        way = self.way
        if way.use_outer:
            for a in range(way.arrays):
                self.wait_swap(a, index, 1)
                slot = self.acc[a].at[index, 1]
                terms = [self.part(a, index, outer_flip=1)] + ([slot] if way.use_core else [])
                sum_rows(slot, terms)
                self.send(slot, self.cross[a].at[index], self.outer, (a, index), self.links.across())

    def terms(self, a, index):
        way = self.way
        self.wait_swap(a, index, 0)
        terms = [self.part(a, index)] + ([self.acc[a].at[index, 0]] if way.use_core else [])
        if way.use_outer:
            slot = self.cross[a].at[index]
            remote(slot, slot, self.outer, (a, index), self.links.across()).wait_recv()
            terms.append(slot)
        return terms

    def halves(self, a):
        low, rows = self.way.splits[a], self.acc[a].shape[2]
        parts = []
        if low > 0:
            parts.append((0, pl.ds(0, low)))
        if low < rows:
            parts.append((1, pl.ds(low, rows - low)))
        return parts

    def toward(self, direction):
        return self.links.down() if direction == 0 else self.links.up()

    def opposite(self):
        way = self.way
        if len(way.distances) % 2:
            return
        index = len(way.distances) - 1
        for a in range(way.arrays):
            sum_rows(self.acc[a].at[index, 0], self.terms(a, index))
            for side, rows in self.halves(a):
                self.send(
                    self.acc[a].at[index, 0].at[rows], self.land[a].at[side, way.steps].at[rows],
                    self.ring, (side, a, way.steps + 1), self.toward(side),
                )

    def wait_land(self, a, side, step, rows=None):
        slot = self.land[a].at[side, step - 1]
        if rows is not None:
            slot = slot.at[rows]
        remote(slot, slot, self.ring, (side, a, step), self.toward(side)).wait_recv()
        return slot

    def step(self, step):
        way = self.way
        for side in range(2):
            index = 2 * step - 1 + side
            for a in range(way.arrays):
                slot = self.acc[a].at[index, 0]
                terms = self.terms(a, index)
                if step < way.steps:
                    terms.append(self.wait_land(a, side, step + 1))
                    sum_rows(slot, terms)
                elif len(way.distances) % 2 == 0:
                    sum_rows(slot, terms)
                    for half, rows in self.halves(a):
                        if half == side:
                            got = self.wait_land(a, side, step + 1, rows)
                            sum_rows(slot.at[rows], [slot.at[rows], got])
                else:
                    sum_rows(slot, terms)
                self.send(
                    slot, self.land[a].at[side, step - 1], self.ring, (side, a, step), self.toward(side)
                )

    def close(self):
        way = self.way
        for a in range(way.arrays):
            terms = self.terms(a, 0) + [self.wait_land(a, side, 1) for side in range(2)]
            if way.use_core and not way.use_outer:
                slot = self.acc[a].at[0, 0]
                sum_rows(slot, terms)
                self.send(slot, self.other[a].at[0], self.last_outer, (a,), self.links.across())
            else:
                slot = self.total[a].at[way.share(self.links)]
                sum_rows(slot, terms)
                if way.use_outer:
                    self.send(slot, slot, self.last_outer, (a,), self.links.across())
                if way.use_core:
                    self.send(slot, slot, self.last_core, (0, a), self.links.sibling())

    def share_out(self):
        way = self.way
        if not way.use_core:
            return
        for a in range(way.arrays):
            if way.use_outer:
                slot = self.total[a].at[way.share(self.links, outer_flip=1)]
                remote(slot, slot, self.last_outer, (a,), self.links.across()).wait_recv()
                self.send(slot, slot, self.last_core, (1, a), self.links.sibling())
            else:
                other = self.other[a].at[0]
                remote(other, other, self.last_outer, (a,), self.links.across()).wait_recv()
                slot = self.total[a].at[way.share(self.links)]
                sum_rows(slot, [self.acc[a].at[0, 0], other])
                self.send(slot, slot, self.last_core, (0, a), self.links.sibling())

    def finish(self, outs):
        way = self.way
        if way.use_core:
            for a in range(way.arrays):
                for o in range(way.outers):
                    slot = self.total[a].at[way.share(self.links, outer_flip=o, core_flip=1)]
                    remote(slot, slot, self.last_core, (o, a), self.links.sibling()).wait_recv()
        for a in range(way.arrays):
            for share in range(way.shares):
                sum_rows(outs[a].at[share], [self.total[a].at[share]])
        for copy in self.pending:
            copy.wait_send()


def reduce_kernel(ways, tp_count, grp_count, *refs):
    links = Links(tp_count, grp_count)
    arrays = sum(way.arrays for way in ways)
    parts, outs, scratch = refs[:arrays], refs[arrays : 2 * arrays], refs[2 * arrays :]
    reduces, at, low = [], 0, 0
    for way in ways:
        count = Reduce.scratch_count(way)
        reduces.append((Reduce(way, links, parts[at : at + way.arrays], scratch[low : low + count]), outs[at : at + way.arrays]))
        at += way.arrays
        low += count
    links.greet(any(w.use_core for w in ways), True, any(w.use_core for w in ways))
    only = [r for r, _ in reduces]
    for index in only[0].order():
        for reduce in only:
            reduce.swap(index)
    for index in only[0].order():
        for reduce in only:
            reduce.crossing(index)
    for reduce in only:
        reduce.opposite()
    for step in range(only[0].way.steps, 0, -1):
        for reduce in only:
            reduce.step(step)
    for reduce in only:
        reduce.close()
    for reduce in only:
        reduce.share_out()
    for reduce, out in reduces:
        reduce.finish(out)


def reduce_weights(ways, parts, tp_count, grp_count, collective_id):
    width = parts[0].shape[-1]
    rows = [x.shape[2] for x in parts]
    scratch, at = [], 0
    for way in ways:
        scratch += Reduce.scratch(way, rows[at : at + way.arrays], width)
        at += way.arrays
    vmem = pl.BlockSpec(memory_space=pltpu.VMEM)
    return pl.pallas_call(
        functools.partial(reduce_kernel, ways, tp_count, grp_count),
        in_specs=[vmem] * len(parts),
        out_specs=[vmem] * len(parts),
        out_shape=[jax.ShapeDtypeStruct(x.shape[1:], F32) for x in parts],
        scratch_shapes=scratch,
        compiler_params=pltpu.CompilerParams(collective_id=collective_id, has_side_effects=True),
    )(*parts)


def softmax_of(q, k, key_bias):
    scores = dot(q, k, NT) * SCALE + key_bias
    exps = jnp.exp(scores - jnp.max(scores, axis=-1, keepdims=True))
    return exps / jnp.sum(exps, axis=-1, keepdims=True)


def attend_kernel(images, x_ref, qk_ref, vo_ref, qkb_ref, vb_ref, key_ref, qk_out, v_out, o_out, acc_ref):
    rows = x_ref.shape[0] // images
    x = x_ref[...]
    qk = (dot(x, qk_ref[0, 0], NT) + qkb_ref[0, 0]).astype(BF16)
    v = (dot(x, vo_ref[0, 0, 0], NT) + vb_ref[0, 0]).astype(BF16)
    qk_out[0, 0] = qk
    v_out[0, 0] = v
    for image in range(images):
        span = slice(image * rows, (image + 1) * rows)
        probs = softmax_of(qk[span, :HEAD_DIM], qk[span, HEAD_DIM:], key_ref[image])
        o_out[0, 0, span, :] = dot(probs.astype(BF16), v[span], NN).astype(BF16)
    update = dot(o_out[0, 0], vo_ref[0, 1, 0], NN)

    @pl.when(pl.program_id(0) == 0)
    def _():
        acc_ref[...] = update

    @pl.when(pl.program_id(0) > 0)
    def _():
        acc_ref[...] += update


def head_specs(local):
    whole = lambda *shape: pl.BlockSpec(shape, lambda h: (0,) * len(shape))
    per_head = lambda *shape: pl.BlockSpec(
        (1, 1) + shape, lambda h: (h // local, h % local) + (0,) * len(shape)
    )
    pair = lambda *shape: pl.BlockSpec(
        (1, 2, 1) + shape, lambda h: (h // local, 0, h % local) + (0,) * len(shape)
    )
    return whole, per_head, pair


def attend(attn_in, w_qk, w_vo, qk_bias, v_bias, key_bias):
    shards, local, _, width = w_qk.shape
    rows = attn_in.shape[0]
    images, _, cap = key_bias.shape
    whole, per_head, pair = head_specs(local)
    return pl.pallas_call(
        functools.partial(attend_kernel, images),
        grid=(shards * local,),
        in_specs=[
            whole(rows, width),
            per_head(2 * HEAD_DIM, width),
            pair(HEAD_DIM, width),
            per_head(1, 2 * HEAD_DIM),
            per_head(1, HEAD_DIM),
            whole(images, 1, cap),
        ],
        out_specs=[
            per_head(rows, 2 * HEAD_DIM),
            per_head(rows, HEAD_DIM),
            per_head(rows, HEAD_DIM),
            whole(rows, width),
        ],
        out_shape=[
            jax.ShapeDtypeStruct((shards, local, rows, 2 * HEAD_DIM), BF16),
            jax.ShapeDtypeStruct((shards, local, rows, HEAD_DIM), BF16),
            jax.ShapeDtypeStruct((shards, local, rows, HEAD_DIM), BF16),
            jax.ShapeDtypeStruct((rows, width), F32),
        ],
    )(attn_in, w_qk, w_vo, qk_bias, v_bias, key_bias)


def attend_back_kernel(
    images, x_ref, grad_ref, qkw_ref, vow_ref, qk_ref, v_ref, o_ref, key_ref,
    dqkw_ref, dvow_ref, dqkb_ref, dvb_ref, dx_ref, dqk_ref, dv_ref,
):
    rows = x_ref.shape[0] // images
    grad_out = dot(grad_ref[...], vow_ref[0, 1, 0], NT).astype(BF16)
    for image in range(images):
        span = slice(image * rows, (image + 1) * rows)
        q, k = qk_ref[0, 0, span, :HEAD_DIM], qk_ref[0, 0, span, HEAD_DIM:]
        probs = softmax_of(q, k, key_ref[image])
        gout = grad_out[span]
        grad_probs = dot(gout, v_ref[0, 0, span, :], NT)
        inner = jnp.sum(probs * grad_probs, axis=-1, keepdims=True)
        grad_scores = (probs * (grad_probs - inner)).astype(BF16)
        dqk_ref[span, :HEAD_DIM] = (dot(grad_scores, k, NN) * SCALE).astype(BF16)
        dqk_ref[span, HEAD_DIM:] = (dot(grad_scores, q, TN) * SCALE).astype(BF16)
        dv_ref[span, :] = dot(probs.astype(BF16), gout, TN).astype(BF16)

    dqk, dv, x = dqk_ref[...], dv_ref[...], x_ref[...]
    dqkw_ref[0, 0] = dot(dqk, x, TN).astype(BF16)
    dvow_ref[0, 0, 0] = dot(dv, x, TN).astype(BF16)
    dvow_ref[0, 1, 0] = dot(o_ref[0, 0], grad_ref[...], TN).astype(BF16)
    dqkb_ref[0, 0] = jnp.sum(dqk.astype(F32), axis=0, keepdims=True)
    dvb_ref[0, 0] = jnp.sum(dv.astype(F32), axis=0, keepdims=True)
    update = dot(dqk, qkw_ref[0, 0], NN) + dot(dv, vow_ref[0, 0, 0], NN)

    @pl.when(pl.program_id(0) == 0)
    def _():
        dx_ref[...] = update

    @pl.when(pl.program_id(0) > 0)
    def _():
        dx_ref[...] += update


def attend_back(attn_in, grad_rows, w_qk, w_vo, qk, v, attn_out, key_bias):
    shards, local, _, width = w_qk.shape
    rows = attn_in.shape[0]
    images, _, cap = key_bias.shape
    whole, per_head, pair = head_specs(local)
    return pl.pallas_call(
        functools.partial(attend_back_kernel, images),
        grid=(shards * local,),
        in_specs=[
            whole(rows, width),
            whole(rows, width),
            per_head(2 * HEAD_DIM, width),
            pair(HEAD_DIM, width),
            per_head(rows, 2 * HEAD_DIM),
            per_head(rows, HEAD_DIM),
            per_head(rows, HEAD_DIM),
            whole(images, 1, cap),
        ],
        out_specs=[
            per_head(2 * HEAD_DIM, width),
            pair(HEAD_DIM, width),
            per_head(1, 2 * HEAD_DIM),
            per_head(1, HEAD_DIM),
            whole(rows, width),
        ],
        out_shape=[
            jax.ShapeDtypeStruct((shards, local, 2 * HEAD_DIM, width), BF16),
            jax.ShapeDtypeStruct((shards, 2, local, HEAD_DIM, width), BF16),
            jax.ShapeDtypeStruct((shards, local, 1, 2 * HEAD_DIM), F32),
            jax.ShapeDtypeStruct((shards, local, 1, HEAD_DIM), F32),
            jax.ShapeDtypeStruct((rows, width), F32),
        ],
        scratch_shapes=[pltpu.VMEM((rows, 2 * HEAD_DIM), BF16), pltpu.VMEM((rows, HEAD_DIM), BF16)],
    )(attn_in, grad_rows, w_qk, w_vo, qk, v, attn_out, key_bias)


def layer_stats(values):
    centred = values - jnp.mean(values, axis=-1, keepdims=True)
    inv_std = lax.rsqrt(jnp.mean(centred * centred, axis=-1, keepdims=True) + 1e-06)
    return (centred * inv_std, inv_std)


def layer_back(grad_norm, normed, inv_std):
    mean_grad = jnp.mean(grad_norm, axis=-1, keepdims=True)
    mean_proj = jnp.mean(grad_norm * normed, axis=-1, keepdims=True)
    return inv_std * (grad_norm - mean_grad - normed * mean_proj)


def gelu_both(values):
    coef = (2.0 / jnp.pi) ** 0.5
    square = values * values
    tanh = jnp.tanh(coef * values * (1.0 + 0.044715 * square))
    act = 0.5 * values * (1.0 + tanh)
    slope = 0.5 * (1.0 + tanh) + 0.5 * values * (1.0 - tanh * tanh) * coef * (
        1.0 + 3 * 0.044715 * square
    )
    return act, slope


def shift_grp(x, shift, count):
    return lax.ppermute(x, "grp", [((g + shift) % count, g) for g in range(count)])


def body(
    tokens, cond, keep_counts, orders, ada_weight, ada_bias, qkv_weight, qv_bias,
    out_weight, out_bias, fc1_weight, fc1_bias, fc2_weight, fc2_bias, cotangent,
):
    tp_rank = lax.axis_index("tp")
    grp_rank = lax.axis_index("grp")
    tp_count = lax.axis_size("tp")
    grp_count = lax.axis_size("grp")
    img_dev, tok_count, width = tokens.shape
    img_group = cond.shape[0]
    part = width // tp_count
    hidden = fc1_bias.shape[0]
    local = part // HEAD_DIM
    cap = 3 * tok_count // 4
    row_count = img_dev * cap

    split = grp_count == 4 and local % 2 == 0
    own_b = local // 2 if split else local
    rows_b = hidden * 4 // 9
    rows_x = hidden - rows_b
    if split:
        rows_b, rows_x = rows_b // 2, rows_x // 4
    way = lambda outer, low: Way(tp_count, grp_count, split, split and outer, [low])
    head_ways = [way(True, own_b * HEAD_DIM // 32 * 16), way(False, own_b * 5 * HEAD_DIM // 72 * 16)]
    ff_ways = [way(True, rows_x // 32 * 16), way(False, rows_b * 5 // 128 * 16)]
    share_x = grp_rank if split else 0
    share_b = grp_rank % 2 if split else 0
    pick = lambda x, share: lax.dynamic_index_in_dim(x, share, 0, keepdims=False)

    qkv_rows = qkv_weight.reshape(width, 3, part)
    vo = jnp.stack([qkv_rows[:, 2].T, out_weight]).reshape(-1, 2 * part // head_ways[0].shares, width)
    qk = qkv_rows[:, :2].reshape(width, 2, local, HEAD_DIM).transpose(2, 1, 3, 0)
    qk = qk.reshape(head_ways[1].shares, -1, width)
    ff_x = rows_x * ff_ways[0].shares
    pieces = [[pick(vo, share_x)], [pick(qk, share_b)]]
    for weight in (fc1_weight.T, fc2_weight):
        pieces.append([pick(weight[:ff_x].reshape(-1, rows_x, width), share_x)])
        pieces.append([pick(weight[ff_x:].reshape(-1, rows_b, width), share_b)])
    if split:
        gathered = gather_weights(
            head_ways + ff_ways + ff_ways, [2, 2, 2], pieces, tp_count, grp_count, 0
        )
    else:
        gathered = [lax.all_gather(x[None], "tp") for p in pieces for x in p]
    w_vo, w_qk, w1x, w1b, w2x, w2b = gathered
    w_vo = w_vo.reshape(tp_count, 2, local, HEAD_DIM, width)
    w_qk = w_qk.reshape(tp_count, local, 2 * HEAD_DIM, width)
    flat = lambda x: x.reshape(-1, width)

    own_orders = lax.dynamic_slice_in_dim(orders, tp_rank * img_dev, img_dev, 0)[:, :cap]
    own_counts = lax.dynamic_slice_in_dim(keep_counts, tp_rank * img_dev, img_dev, 0)
    slot = lax.broadcasted_iota(jnp.int32, (img_dev, cap), 1)
    kept = slot < own_counts[:, None]
    place_ids = lax.broadcasted_iota(jnp.int32, (1, 1, tok_count), 2)
    chosen = ((own_orders[:, :, None] == place_ids) & kept[:, :, None]).astype(BF16)
    take = lambda x: jnp.einsum("ijt,itd->ijd", chosen, x, preferred_element_type=F32)
    put = lambda x: jnp.einsum("ijt,ijd->itd", chosen, x.astype(BF16), preferred_element_type=F32)
    key_bias = jnp.where(kept, 0.0, -1e30).astype(F32)[:, None, :]
    keep_col = kept.astype(F32)[:, :, None]

    silu_cond = jax.nn.silu(cond.astype(F32)).astype(BF16)
    ada_cols = (
        jnp.einsum("id,dke->ike", silu_cond, ada_weight, preferred_element_type=F32)
        + ada_bias.astype(F32)[None]
    )
    biases = jnp.concatenate([fc1_bias, qv_bias.reshape(-1)]).astype(F32)
    mod_len = img_dev * 6 * part
    message = jnp.concatenate(
        [
            ada_cols.reshape(tp_count, mod_len),
            jnp.broadcast_to(biases[None], (tp_count, biases.shape[0])),
        ],
        axis=1,
    )
    message = lax.all_to_all(message, "tp", split_axis=0, concat_axis=0, tiled=True)
    modulation = message[:, :mod_len].reshape(tp_count, img_dev, 6, part)
    modulation = modulation.transpose(1, 2, 0, 3).reshape(img_dev, 6, width)
    shift_one, scale_one, gate_one, shift_two, scale_two, gate_two = (
        modulation[:, j][:, None, :] for j in range(6)
    )
    b1 = message[:, mod_len : mod_len + hidden]
    b1x, b1b = b1[:, :ff_x].reshape(-1, 1), b1[:, ff_x:].reshape(-1, 1)
    qv = message[:, mod_len + hidden :].reshape(tp_count, 2, local, 1, HEAD_DIM)
    qk_bias = jnp.concatenate([qv[:, 0], jnp.zeros_like(qv[:, 0])], axis=-1)
    v_bias = qv[:, 1]

    resid = take(tokens)
    grad_out = take(cotangent)
    normed_one, inv_one = layer_stats(resid)
    attn_in = (normed_one * (1.0 + scale_one) + shift_one).astype(BF16).reshape(row_count, width)
    qk, v, attn_out, branch_one = attend(attn_in, w_qk, w_vo, qk_bias, v_bias, key_bias)
    branch_one = branch_one.reshape(img_dev, cap, width) + out_bias.astype(F32)
    delta_one = keep_col * gate_one * branch_one
    hidden_res = resid + delta_one
    normed_two, inv_two = layer_stats(hidden_res)
    mlp_in = (normed_two * (1.0 + scale_two) + shift_two).astype(BF16).reshape(row_count, width)
    grad_two = (grad_out * gate_two).astype(BF16).reshape(row_count, width)
    halves = [(w1x, w2x, b1x), (w1b, w2b, b1b)]
    acts, slopes = [], []
    for w1, _, bias in halves:
        act, slope = gelu_both(dot(flat(w1), mlp_in, NT) + bias)
        acts.append(act.astype(BF16))
        slopes.append(slope.astype(BF16))
    branch_two = sum(dot(act, flat(w2), TN) for act, (_, w2, _) in zip(acts, halves))
    branch_two = branch_two.reshape(img_dev, cap, width) + fc2_bias.astype(F32)
    delta_two = keep_col * gate_two * branch_two
    block_out = tokens.astype(F32) + put(delta_one + delta_two)
    gate_grad_two = jnp.sum(grad_out * branch_two, axis=1)

    ff_parts, grads_pre = [], []
    for act, slope, (w1, w2, _) in zip(acts, slopes, halves):
        grad_pre = (dot(flat(w2), grad_two, NT) * slope.astype(F32)).astype(BF16)
        grads_pre.append(grad_pre)
        ff_parts.append(dot(act, grad_two, NN).astype(BF16).reshape(w2.shape))
    for grad_pre, (w1, _, _) in zip(grads_pre, halves):
        ff_parts.append(dot(grad_pre, mlp_in, NN).astype(BF16).reshape(w1.shape))
    fc1b_part = jnp.concatenate(
        [jnp.sum(g.astype(F32), axis=1).reshape(tp_count, -1) for g in grads_pre], axis=1
    )
    fc2b_part = jnp.sum(grad_two.astype(F32), axis=0)
    grad_mlp_in = sum(dot(g, flat(w1), TN) for g, (w1, _, _) in zip(grads_pre, halves))
    grad_mlp_in = grad_mlp_in.reshape(img_dev, cap, width)
    shift_grad_two = jnp.sum(grad_mlp_in, axis=1)
    scale_grad_two = jnp.sum(grad_mlp_in * normed_two, axis=1)
    back_two = layer_back(grad_mlp_in * (1.0 + scale_two), normed_two, inv_two)
    grad_hidden = grad_out + back_two
    gate_grad_one = jnp.sum(grad_hidden * keep_col * branch_one, axis=1)
    grad_one = (grad_hidden * keep_col * gate_one).astype(BF16).reshape(row_count, width)
    outb_part = jnp.sum(grad_one.astype(F32), axis=0)
    dqk, dvo, dqk_bias, dv_bias, grad_attn_in = attend_back(
        attn_in, grad_one, w_qk, w_vo, qk, v, attn_out, key_bias
    )
    head_parts = [
        dvo.reshape(tp_count, head_ways[0].shares, -1, width),
        dqk.reshape(tp_count, head_ways[1].shares, -1, width),
    ]
    if split:
        ff_sums = reduce_weights(ff_ways + ff_ways, ff_parts, tp_count, grp_count, 1)
        head_sums = reduce_weights(head_ways, head_parts, tp_count, grp_count, 2)
    else:
        scatter = lambda x: lax.psum_scatter(x, "tp", scatter_dimension=0)
        ff_sums, head_sums = (
            [lax.psum(scatter(x), "grp").astype(F32) for x in parts]
            for parts in (ff_parts, head_parts)
        )
    fc2_sum = jnp.concatenate([flat(ff_sums[0]), flat(ff_sums[1])])
    fc1_sum = jnp.concatenate([flat(ff_sums[2]), flat(ff_sums[3])])
    v_sum, out_sum = flat(head_sums[0])[:part], flat(head_sums[0])[part:]
    qk_sum = head_sums[1].reshape(local, 2, HEAD_DIM, width).transpose(1, 0, 2, 3)
    qkv_sum = jnp.concatenate([qk_sum.reshape(2, part, width), v_sum[None]]).transpose(2, 0, 1)

    grad_attn_in = grad_attn_in.reshape(img_dev, cap, width)
    shift_grad_one = jnp.sum(grad_attn_in, axis=1)
    scale_grad_one = jnp.sum(grad_attn_in * normed_one, axis=1)
    back_one = layer_back(grad_attn_in * (1.0 + scale_one), normed_one, inv_one)
    grad_tokens = cotangent.astype(F32) + put(back_two + back_one)

    modulation_grad = jnp.stack(
        [
            shift_grad_one, scale_grad_one, gate_grad_one,
            shift_grad_two, scale_grad_two, gate_grad_two,
        ],
        axis=1,
    )
    mod_rows = modulation_grad.reshape(img_dev, 6, tp_count, part).transpose(2, 0, 1, 3)
    message = jnp.concatenate(
        [
            mod_rows.reshape(tp_count, mod_len),
            fc1b_part,
            dqk_bias[..., :HEAD_DIM].reshape(tp_count, part),
            dv_bias.reshape(tp_count, part),
            outb_part.reshape(tp_count, part),
            fc2b_part.reshape(tp_count, part),
        ],
        axis=1,
    )
    message = lax.all_to_all(message, "tp", split_axis=0, concat_axis=0, tiled=True)
    grad_cols = message[:, :mod_len].reshape(img_group, 6, part).astype(BF16)
    bias_sums = jnp.sum(message[:, mod_len:], axis=0)
    shifts = range(1, grp_count)
    around = lambda x: [x] + [shift_grp(x, k, grp_count) for k in shifts]
    cols_all = jnp.concatenate(around(grad_cols), 0)
    silu_all = jnp.concatenate(around(silu_cond), 0)
    bias_sums = sum(around(bias_sums))
    kept_int = jnp.sum(sum(around(keep_counts)))
    kept_total = kept_int.astype(F32)
    ada_sum = jnp.einsum("id,ike->dke", silu_all, cols_all, preferred_element_type=F32)
    adab_sum = jnp.sum(cols_all.astype(F32), axis=0)
    cond_part = jnp.einsum("ike,dke->id", grad_cols, ada_weight, preferred_element_type=F32)
    cond_part = cond_part.astype(BF16).reshape(img_group, tp_count, part).transpose(1, 0, 2)
    cond_rows = lax.all_to_all(
        cond_part.reshape(tp_count, img_group * part), "tp", split_axis=0, concat_axis=0, tiled=True
    )
    cond_sum = jnp.sum(cond_rows.astype(F32), axis=0).reshape(img_group, part)
    cond_cols = lax.dynamic_slice_in_dim(cond, tp_rank * part, part, 1).astype(F32)
    cond_grad = jax.vjp(jax.nn.silu, cond_cols)[1](cond_sum)[0]

    all_tokens = img_group * tok_count * grp_count
    token_counts = jnp.stack([kept_int, all_tokens - kept_int]).astype(jnp.int32)
    at = [0, hidden, hidden + 2 * part, hidden + 3 * part, hidden + 4 * part]
    fc1b_sum, qvb_sum, outb_sum, fc2b_sum = (bias_sums[a:b] for a, b in zip(at, at[1:]))
    scaled = lambda x: x.astype(F32) / kept_total
    return (
        block_out,
        grad_tokens,
        cond_grad,
        scaled(ada_sum),
        scaled(adab_sum),
        scaled(qkv_sum),
        scaled(qvb_sum.reshape(2, part)),
        scaled(out_sum),
        scaled(outb_sum),
        scaled(fc1_sum.T),
        scaled(fc1b_sum),
        scaled(fc2_sum),
        scaled(fc2b_sum),
        token_counts,
    )


def solution(mesh):
    in_specs = (
        P(("grp", "tp"), None, None),
        P("grp", None),
        P("grp"),
        P("grp", None),
        P(None, None, "tp"),
        P(None, "tp"),
        P(None, None, "tp"),
        P(None, "tp"),
        P("tp", None),
        P(),
        P(None, "tp"),
        P("tp"),
        P("tp", None),
        P(),
        P(("grp", "tp"), None, None),
    )
    out_specs = (
        P(("grp", "tp"), None, None),
        P(("grp", "tp"), None, None),
        P("grp", "tp"),
        P(None, None, "tp"),
        P(None, "tp"),
        P(None, None, "tp"),
        P(None, "tp"),
        P("tp", None),
        P("tp"),
        P(None, "tp"),
        P("tp"),
        P("tp", None),
        P("tp"),
        P(),
    )
    return jax.shard_map(body, mesh=mesh, in_specs=in_specs, out_specs=out_specs, check_vma=False)
```

```python
import functools

import jax
import jax.numpy as jnp
from jax import lax
from jax.experimental import pallas as pl
from jax.experimental.pallas import tpu as pltpu
from jax.sharding import PartitionSpec as P

HEAD_DIM = 72
SCALE = HEAD_DIM ** (-0.5)
F32 = jnp.float32
BF16 = jnp.bfloat16
NT = (((1,), (1,)), ((), ()))
NN = (((1,), (0,)), ((), ()))
TN = (((0,), (0,)), ((), ()))


def dot(a, b, dims):
    return lax.dot_general(a, b, dims, preferred_element_type=F32)


MESH = pl.DeviceIdType.MESH


class Links:
    def __init__(self, tp_count, grp_count):
        self.tp_count = tp_count
        self.cores = 2 if grp_count % 2 == 0 else 1
        self.outer = grp_count // self.cores
        self.steps = (tp_count - 1) // 2
        self.tp = lax.axis_index("tp")
        self.grp = lax.axis_index("grp")
        self.core = self.grp % self.cores
        half = (tp_count + 1) // 2
        self.half = half
        tp = self.tp
        self.place = jnp.where(tp % 2 == 0, tp // 2, half + (tp_count - 1 - tp) // 2)

    def shard(self, distance):
        ring = (self.place + distance + self.tp_count) % self.tp_count
        return jnp.where(ring < self.half, 2 * ring, 2 * (self.tp_count - 1 - ring) + 1)

    def up(self):
        return (self.grp, self.shard(1))

    def down(self):
        return (self.grp, self.shard(-1))

    def sibling(self):
        return (self.grp + 1 - 2 * self.core, self.tp)

    def across(self):
        return ((self.grp + self.cores) % (self.cores * self.outer), self.tp)

    def greet(self, use_core, use_outer, split=True):
        peers = [self.up(), self.down()]
        if use_core:
            peers.append(self.sibling())
        if use_outer and split:
            peers.append(self.across())
        barrier = pltpu.get_barrier_semaphore()
        for peer in peers:
            pl.semaphore_signal(barrier, inc=1, device_id=peer, device_id_type=MESH)
        pl.semaphore_wait(barrier, len(peers))


class Way:
    def __init__(self, tp_count, grp_count, use_core, use_outer, splits):
        self.cores = 2 if use_core else 1
        self.outers = 2 if use_outer else 1
        self.use_core, self.use_outer = use_core, use_outer
        self.shares = self.cores * self.outers
        self.splits = splits
        self.steps = (tp_count - 1) // 2
        self.distances = [0] + [s * d for d in range(1, self.steps + 1) for s in (-1, 1)]
        if tp_count % 2 == 0:
            self.distances.append(tp_count // 2)
        self.arrays = len(splits)

    def share(self, links, outer_flip=0, core_flip=0):
        share = 0
        if self.use_outer:
            share = (links.grp // links.cores + outer_flip) % 2
        if self.use_core:
            share = share * 2 + (links.core + core_flip) % 2
        return share


def remote(src, dst, sems, index, device):
    return pltpu.make_async_remote_copy(
        src_ref=src, dst_ref=dst, send_sem=sems[0].at[index], recv_sem=sems[1].at[index],
        device_id=device, device_id_type=MESH,
    )


def sem_pair(*shape):
    return [pltpu.SemaphoreType.DMA(shape), pltpu.SemaphoreType.DMA(shape)]


class Gather:
    @staticmethod
    def scratch(way):
        n, a = len(way.distances), way.arrays
        shapes = sem_pair(2, a, way.steps + 2)
        shapes += sem_pair(a, n) + sem_pair(2, a, n)
        return shapes + [pltpu.SemaphoreType.DMA((a,))]

    def __init__(self, way, links, own, full, scratch):
        self.way, self.links, self.own, self.full = way, links, own, full
        self.ring, self.outer, self.core = scratch[0:2], scratch[2:4], scratch[4:6]
        self.local = scratch[6]
        self.pending = []

    def slot(self, a, index, **flips):
        way = self.way
        return self.full[a].at[self.links.shard(way.distances[index]), way.share(self.links, **flips)]

    def hop(self, a, index, direction, step, src=None, rows=None):
        src = self.slot(a, index) if src is None else src
        dst = self.slot(a, index)
        if rows is not None:
            src, dst = src.at[rows], dst.at[rows]
        device = self.links.up() if direction == 0 else self.links.down()
        return remote(src, dst, self.ring, (direction, a, step), device)

    def spread(self, a, index, src=None):
        src = self.slot(a, index) if src is None else src
        if self.way.use_outer:
            copy = remote(src, self.slot(a, index), self.outer, (a, index), self.links.across())
            copy.start()
            self.pending.append(copy)
        if self.way.use_core:
            copy = remote(src, self.slot(a, index), self.core, (0, a, index), self.links.sibling())
            copy.start()
            self.pending.append(copy)

    def relay(self, index):
        if not self.way.use_outer:
            return
        for a in range(self.way.arrays):
            slot = self.slot(a, index, outer_flip=1)
            remote(slot, slot, self.outer, (a, index), self.links.across()).wait_recv()
            if self.way.use_core:
                copy = remote(slot, slot, self.core, (1, a, index), self.links.sibling())
                copy.start()
                self.pending.append(copy)

    def halves(self, a):
        low = self.way.splits[a]
        rows = self.own[a].shape[0]
        parts = []
        if low > 0:
            parts.append((0, pl.ds(0, low)))
        if low < rows:
            parts.append((1, pl.ds(low, rows - low)))
        return parts

    def start(self):
        for a in range(self.way.arrays):
            for direction in range(2):
                copy = self.hop(a, 0, direction, 1, src=self.own[a])
                copy.start()
                self.pending.append(copy)
        for a in range(self.way.arrays):
            self.spread(a, 0, src=self.own[a])
            copy = pltpu.make_async_copy(self.own[a], self.slot(a, 0), self.local.at[a])
            copy.start()

    def round(self, step):
        way = self.way
        if step <= way.steps:
            for a in range(way.arrays):
                for direction in range(2):
                    index = 2 * step - 1 + direction
                    self.hop(a, index, direction, step).wait_recv()
                    if step < way.steps:
                        copy = self.hop(a, index, direction, step + 1)
                        copy.start()
                        self.pending.append(copy)
                    elif len(way.distances) % 2 == 0:
                        for side, rows in self.halves(a):
                            if side == direction:
                                copy = self.hop(a, index, direction, step + 1, rows=rows)
                                copy.start()
                                self.pending.append(copy)
            for a in range(way.arrays):
                for direction in range(2):
                    self.spread(a, 2 * step - 1 + direction)
        else:
            last = len(way.distances) - 1
            for a in range(way.arrays):
                for side, rows in self.halves(a):
                    self.hop(a, last, side, step, rows=rows).wait_recv()
                self.spread(a, last)

    def rounds(self):
        return self.way.steps + (1 if len(self.way.distances) % 2 == 0 else 0)

    def tail(self):
        for index in range(max(0, 2 * self.rounds() - 3), len(self.way.distances)):
            self.relay(index)

    def finish(self):
        way = self.way
        for a in range(way.arrays):
            pltpu.make_async_copy(self.own[a], self.slot(a, 0), self.local.at[a]).wait()
        if way.use_core:
            for index in range(len(way.distances)):
                for a in range(way.arrays):
                    for o in range(way.outers):
                        slot = self.slot(a, index, outer_flip=o, core_flip=1)
                        remote(slot, slot, self.core, (o, a, index), self.links.sibling()).wait_recv()
        for copy in self.pending:
            copy.wait_send()


def gather_kernel(ways, set_sizes, tp_count, grp_count, *refs):
    links = Links(tp_count, grp_count)
    arrays = sum(way.arrays for way in ways)
    own, full, scratch = refs[:arrays], refs[arrays : 2 * arrays], refs[2 * arrays :]
    gathers, at = [], 0
    for i, way in enumerate(ways):
        gathers.append(
            Gather(way, links, own[at : at + way.arrays], full[at : at + way.arrays], scratch[7 * i : 7 * i + 7])
        )
        at += way.arrays
    links.greet(any(w.use_core for w in ways), any(w.use_outer for w in ways))
    sets, at = [], 0
    for size in set_sizes:
        sets.append(gathers[at : at + size])
        at += size
    for gather in sets[0]:
        gather.start()
    for i, group in enumerate(sets):
        rounds, steps = group[0].rounds(), group[0].way.steps
        for step in range(1, rounds + 1):
            for gather in group:
                gather.round(step)
            if step == steps and i + 1 < len(sets):
                for gather in sets[i + 1]:
                    gather.start()
            for gather in group:
                for index in [0] if step == 2 else [2 * step - 5, 2 * step - 4] if step > 2 else []:
                    gather.relay(index)
            if step == 1 and i > 0:
                for gather in sets[i - 1]:
                    gather.tail()
    for gather in sets[-1]:
        gather.tail()
    for gather in gathers:
        gather.finish()


def gather_weights(ways, set_sizes, pieces, tp_count, grp_count, collective_id):
    arrays = [x for p in pieces for x in p]
    shares = [way.shares for way in ways for _ in range(way.arrays)]
    out = pl.pallas_call(
        functools.partial(gather_kernel, ways, set_sizes, tp_count, grp_count),
        in_specs=[pl.BlockSpec(memory_space=pltpu.VMEM)] * len(arrays),
        out_specs=[pl.BlockSpec(memory_space=pltpu.HBM)] * len(arrays),
        out_shape=[
            jax.ShapeDtypeStruct((tp_count, s) + x.shape, x.dtype) for s, x in zip(shares, arrays)
        ],
        scratch_shapes=[s for way in ways for s in Gather.scratch(way)],
        compiler_params=pltpu.CompilerParams(collective_id=collective_id, has_side_effects=True),
    )(*arrays)
    return out


def sum_rows(target, terms):
    rows = target.shape[0]

    def some(span):
        total = terms[0][span, :].astype(F32)
        for term in terms[1:]:
            total = total + term[span, :].astype(F32)
        target[span, :] = total.astype(target.dtype)

    whole = rows // 16

    def step(i, carry):
        some(pl.ds(pl.multiple_of(i * 16, 16), 16))
        return carry

    lax.fori_loop(0, whole, step, 0)
    if rows % 16:
        some(pl.ds(whole * 16, rows % 16))


class Reduce:
    @staticmethod
    def scratch(way, rows, width):
        n = len(way.distances)
        shapes = []
        for a in range(way.arrays):
            shapes += [
                pltpu.VMEM((n, way.outers, rows[a], width), BF16),
                pltpu.VMEM((n if way.use_outer else 1, rows[a], width), BF16),
                pltpu.VMEM((2, way.steps + 1, rows[a], width), BF16),
                pltpu.VMEM((n, way.outers, rows[a], width), BF16),
                pltpu.VMEM((1, rows[a], width), BF16),
            ]
        a = way.arrays
        shapes += sem_pair(2, a, way.steps + 2) + sem_pair(a, n) + sem_pair(2, a, n)
        return shapes + sem_pair(a) + sem_pair(2, a) + [pltpu.SemaphoreType.DMA((2, a, n))]

    @staticmethod
    def scratch_count(way):
        return 5 * way.arrays + 11

    def __init__(self, way, links, parts, outs, scratch):
        self.way, self.links, self.parts, self.total = way, links, parts, outs
        bufs, sems = scratch[: 5 * way.arrays], scratch[5 * way.arrays :]
        self.acc, self.cross, self.land, self.own, self.other = (bufs[k::5] for k in range(5))
        self.ring, self.outer, self.core = sems[0:2], sems[2:4], sems[4:6]
        self.last_outer, self.last_core = sems[6:8], sems[8:10]
        self.fetched = sems[10]
        self.pending = []

    def part(self, a, index, **flips):
        way = self.way
        return self.parts[a].at[self.links.shard(way.distances[index]), way.share(self.links, **flips)]

    def send(self, src, dst, sems, index, device):
        copy = remote(src, dst, sems, index, device)
        copy.start()
        self.pending.append(copy)

    def order(self):
        return list(range(len(self.way.distances)))[::-1]

    def fetch(self, a, index, o):
        return pltpu.make_async_copy(
            self.part(a, index, outer_flip=o), self.own[a].at[index, o], self.fetched.at[o, a, index]
        )

    def fetch_all(self):
        for index in self.order():
            for o in range(self.way.outers)[::-1]:
                for a in range(self.way.arrays):
                    self.fetch(a, index, o).start()

    def fetched_part(self, a, index, o):
        self.fetch(a, index, o).wait()
        return self.own[a].at[index, o]

    def swap(self, index):
        way = self.way
        if way.use_core:
            for o in range(way.outers)[::-1]:
                for a in range(way.arrays):
                    self.send(
                        self.part(a, index, outer_flip=o, core_flip=1),
                        self.acc[a].at[index, o], self.core, (o, a, index), self.links.sibling(),
                    )

    def wait_swap(self, a, index, o):
        if self.way.use_core:
            slot = self.acc[a].at[index, o]
            remote(slot, slot, self.core, (o, a, index), self.links.sibling()).wait_recv()

    def crossing(self, index):
        way = self.way
        if way.use_outer:
            for a in range(way.arrays):
                self.wait_swap(a, index, 1)
                slot = self.acc[a].at[index, 1]
                terms = [self.fetched_part(a, index, 1)] + ([slot] if way.use_core else [])
                sum_rows(slot, terms)
                self.send(slot, self.cross[a].at[index], self.outer, (a, index), self.links.across())

    def terms(self, a, index):
        way = self.way
        self.wait_swap(a, index, 0)
        terms = [self.fetched_part(a, index, 0)] + ([self.acc[a].at[index, 0]] if way.use_core else [])
        if way.use_outer:
            slot = self.cross[a].at[index]
            remote(slot, slot, self.outer, (a, index), self.links.across()).wait_recv()
            terms.append(slot)
        return terms

    def halves(self, a):
        low, rows = self.way.splits[a], self.acc[a].shape[2]
        parts = []
        if low > 0:
            parts.append((0, pl.ds(0, low)))
        if low < rows:
            parts.append((1, pl.ds(low, rows - low)))
        return parts

    def toward(self, direction):
        return self.links.down() if direction == 0 else self.links.up()

    def opposite(self):
        way = self.way
        if len(way.distances) % 2:
            return
        index = len(way.distances) - 1
        for a in range(way.arrays):
            sum_rows(self.acc[a].at[index, 0], self.terms(a, index))
            for side, rows in self.halves(a):
                self.send(
                    self.acc[a].at[index, 0].at[rows], self.land[a].at[side, way.steps].at[rows],
                    self.ring, (side, a, way.steps + 1), self.toward(side),
                )

    def wait_land(self, a, side, step, rows=None):
        slot = self.land[a].at[side, step - 1]
        if rows is not None:
            slot = slot.at[rows]
        remote(slot, slot, self.ring, (side, a, step), self.toward(side)).wait_recv()
        return slot

    def step(self, step):
        way = self.way
        for side in range(2):
            index = 2 * step - 1 + side
            for a in range(way.arrays):
                slot = self.acc[a].at[index, 0]
                terms = self.terms(a, index)
                if step < way.steps:
                    terms.append(self.wait_land(a, side, step + 1))
                    sum_rows(slot, terms)
                elif len(way.distances) % 2 == 0:
                    sum_rows(slot, terms)
                    for half, rows in self.halves(a):
                        if half == side:
                            got = self.wait_land(a, side, step + 1, rows)
                            sum_rows(slot.at[rows], [slot.at[rows], got])
                else:
                    sum_rows(slot, terms)
                self.send(
                    slot, self.land[a].at[side, step - 1], self.ring, (side, a, step), self.toward(side)
                )

    def close(self):
        way = self.way
        for a in range(way.arrays):
            terms = self.terms(a, 0) + [self.wait_land(a, side, 1) for side in range(2)]
            if way.use_core and not way.use_outer:
                slot = self.acc[a].at[0, 0]
                sum_rows(slot, terms)
                self.send(slot, self.other[a].at[0], self.last_outer, (a,), self.links.across())
            else:
                slot = self.total[a].at[way.share(self.links)]
                sum_rows(slot, terms)
                if way.use_outer:
                    self.send(slot, slot, self.last_outer, (a,), self.links.across())
                if way.use_core:
                    self.send(slot, slot, self.last_core, (0, a), self.links.sibling())

    def share_out(self):
        way = self.way
        if not way.use_core:
            return
        for a in range(way.arrays):
            if way.use_outer:
                slot = self.total[a].at[way.share(self.links, outer_flip=1)]
                remote(slot, slot, self.last_outer, (a,), self.links.across()).wait_recv()
                self.send(slot, slot, self.last_core, (1, a), self.links.sibling())
            else:
                other = self.other[a].at[0]
                remote(other, other, self.last_outer, (a,), self.links.across()).wait_recv()
                slot = self.total[a].at[way.share(self.links)]
                sum_rows(slot, [self.acc[a].at[0, 0], other])
                self.send(slot, slot, self.last_core, (0, a), self.links.sibling())

    def finish(self):
        way = self.way
        if way.use_core:
            for a in range(way.arrays):
                for o in range(way.outers):
                    slot = self.total[a].at[way.share(self.links, outer_flip=o, core_flip=1)]
                    remote(slot, slot, self.last_core, (o, a), self.links.sibling()).wait_recv()
        for copy in self.pending:
            copy.wait_send()


def reduce_kernel(ways, tp_count, grp_count, *refs):
    links = Links(tp_count, grp_count)
    arrays = sum(way.arrays for way in ways)
    parts, outs, scratch = refs[:arrays], refs[arrays : 2 * arrays], refs[2 * arrays :]
    only, at, low = [], 0, 0
    for way in ways:
        count = Reduce.scratch_count(way)
        span = slice(at, at + way.arrays)
        only.append(Reduce(way, links, parts[span], outs[span], scratch[low : low + count]))
        at += way.arrays
        low += count
    for reduce in only:
        reduce.fetch_all()
    links.greet(any(w.use_core for w in ways), True, any(w.use_core for w in ways))
    for stage in reduce_stages(only):
        stage()


def reduce_stages(reduces):
    way = reduces[0].way
    order, steps = reduces[0].order(), way.steps

    def swaps():
        for index in order:
            for reduce in reduces:
                reduce.swap(index)

    def every(name, *args):
        def stage():
            for reduce in reduces:
                getattr(reduce, name)(*args)

        return stage

    stages = [swaps]
    if len(way.distances) % 2 == 0:
        stages.append(every("crossing", order[0]))
    for side in (2 * steps, 2 * steps - 1):
        stages.append(every("crossing", side))
    stages.append(every("opposite"))
    for step in range(steps, 0, -1):
        ahead = [2 * step - 2, 2 * step - 3] if step > 1 else [0]
        for index in ahead:
            stages.append(every("crossing", index))
        stages.append(every("step", step))
    return stages + [every("close"), every("share_out"), every("finish")]


def reduce_weights(ways, parts, tp_count, grp_count, collective_id):
    width = parts[0].shape[-1]
    rows = [x.shape[2] for x in parts]
    scratch, at = [], 0
    for way in ways:
        scratch += Reduce.scratch(way, rows[at : at + way.arrays], width)
        at += way.arrays
    vmem = pl.BlockSpec(memory_space=pltpu.VMEM)
    return pl.pallas_call(
        functools.partial(reduce_kernel, ways, tp_count, grp_count),
        in_specs=[pl.BlockSpec(memory_space=pltpu.HBM)] * len(parts),
        out_specs=[vmem] * len(parts),
        out_shape=[jax.ShapeDtypeStruct(x.shape[1:], BF16) for x in parts],
        scratch_shapes=scratch,
        compiler_params=pltpu.CompilerParams(collective_id=collective_id, has_side_effects=True),
    )(*parts)


def softmax_of(q, k, key_bias):
    scores = dot(q, k, NT) * SCALE + key_bias
    exps = jnp.exp(scores - jnp.max(scores, axis=-1, keepdims=True))
    return exps / jnp.sum(exps, axis=-1, keepdims=True)


def attend_kernel(images, x_ref, qk_ref, vo_ref, qkb_ref, vb_ref, key_ref, qk_out, v_out, o_out, acc_ref):
    rows = x_ref.shape[0] // images
    x = x_ref[...]
    qk = (dot(x, qk_ref[0, 0], NT) + qkb_ref[0, 0]).astype(BF16)
    v = (dot(x, vo_ref[0, 0, 0], NT) + vb_ref[0, 0]).astype(BF16)
    qk_out[0, 0] = qk
    v_out[0, 0] = v
    for image in range(images):
        span = slice(image * rows, (image + 1) * rows)
        probs = softmax_of(qk[span, :HEAD_DIM], qk[span, HEAD_DIM:], key_ref[image])
        o_out[0, 0, span, :] = dot(probs.astype(BF16), v[span], NN).astype(BF16)
    update = dot(o_out[0, 0], vo_ref[0, 1, 0], NN)

    @pl.when(pl.program_id(0) == 0)
    def _():
        acc_ref[...] = update

    @pl.when(pl.program_id(0) > 0)
    def _():
        acc_ref[...] += update


def head_specs(local):
    whole = lambda *shape: pl.BlockSpec(shape, lambda h: (0,) * len(shape))
    per_head = lambda *shape: pl.BlockSpec(
        (1, 1) + shape, lambda h: (h // local, h % local) + (0,) * len(shape)
    )
    pair = lambda *shape: pl.BlockSpec(
        (1, 2, 1) + shape, lambda h: (h // local, 0, h % local) + (0,) * len(shape)
    )
    return whole, per_head, pair


def attend(attn_in, w_qk, w_vo, qk_bias, v_bias, key_bias):
    shards, local, _, width = w_qk.shape
    rows = attn_in.shape[0]
    images, _, cap = key_bias.shape
    whole, per_head, pair = head_specs(local)
    return pl.pallas_call(
        functools.partial(attend_kernel, images),
        grid=(shards * local,),
        in_specs=[
            whole(rows, width),
            per_head(2 * HEAD_DIM, width),
            pair(HEAD_DIM, width),
            per_head(1, 2 * HEAD_DIM),
            per_head(1, HEAD_DIM),
            whole(images, 1, cap),
        ],
        out_specs=[
            per_head(rows, 2 * HEAD_DIM),
            per_head(rows, HEAD_DIM),
            per_head(rows, HEAD_DIM),
            whole(rows, width),
        ],
        out_shape=[
            jax.ShapeDtypeStruct((shards, local, rows, 2 * HEAD_DIM), BF16),
            jax.ShapeDtypeStruct((shards, local, rows, HEAD_DIM), BF16),
            jax.ShapeDtypeStruct((shards, local, rows, HEAD_DIM), BF16),
            jax.ShapeDtypeStruct((rows, width), F32),
        ],
    )(attn_in, w_qk, w_vo, qk_bias, v_bias, key_bias)


def attend_back_kernel(
    images, x_ref, grad_ref, qkw_ref, vow_ref, qk_ref, v_ref, o_ref, key_ref,
    dqkw_ref, dvow_ref, dqkb_ref, dvb_ref, dx_ref, dqk_ref, dv_ref,
):
    rows = x_ref.shape[0] // images
    grad_out = dot(grad_ref[...], vow_ref[0, 1, 0], NT).astype(BF16)
    for image in range(images):
        span = slice(image * rows, (image + 1) * rows)
        q, k = qk_ref[0, 0, span, :HEAD_DIM], qk_ref[0, 0, span, HEAD_DIM:]
        probs = softmax_of(q, k, key_ref[image])
        gout = grad_out[span]
        grad_probs = dot(gout, v_ref[0, 0, span, :], NT)
        inner = jnp.sum(probs * grad_probs, axis=-1, keepdims=True)
        grad_scores = (probs * (grad_probs - inner)).astype(BF16)
        dqk_ref[span, :HEAD_DIM] = (dot(grad_scores, k, NN) * SCALE).astype(BF16)
        dqk_ref[span, HEAD_DIM:] = (dot(grad_scores, q, TN) * SCALE).astype(BF16)
        dv_ref[span, :] = dot(probs.astype(BF16), gout, TN).astype(BF16)

    dqk, dv, x = dqk_ref[...], dv_ref[...], x_ref[...]
    dqkw_ref[0, 0] = dot(dqk, x, TN).astype(BF16)
    dvow_ref[0, 0, 0] = dot(dv, x, TN).astype(BF16)
    dvow_ref[0, 1, 0] = dot(o_ref[0, 0], grad_ref[...], TN).astype(BF16)
    dqkb_ref[0, 0] = jnp.sum(dqk.astype(F32), axis=0, keepdims=True)
    dvb_ref[0, 0] = jnp.sum(dv.astype(F32), axis=0, keepdims=True)
    update = dot(dqk, qkw_ref[0, 0], NN) + dot(dv, vow_ref[0, 0, 0], NN)

    @pl.when(pl.program_id(0) == 0)
    def _():
        dx_ref[...] = update

    @pl.when(pl.program_id(0) > 0)
    def _():
        dx_ref[...] += update


def attend_back(attn_in, grad_rows, w_qk, w_vo, qk, v, attn_out, key_bias):
    shards, local, _, width = w_qk.shape
    rows = attn_in.shape[0]
    images, _, cap = key_bias.shape
    whole, per_head, pair = head_specs(local)
    return pl.pallas_call(
        functools.partial(attend_back_kernel, images),
        grid=(shards * local,),
        in_specs=[
            whole(rows, width),
            whole(rows, width),
            per_head(2 * HEAD_DIM, width),
            pair(HEAD_DIM, width),
            per_head(rows, 2 * HEAD_DIM),
            per_head(rows, HEAD_DIM),
            per_head(rows, HEAD_DIM),
            whole(images, 1, cap),
        ],
        out_specs=[
            per_head(2 * HEAD_DIM, width),
            pair(HEAD_DIM, width),
            per_head(1, 2 * HEAD_DIM),
            per_head(1, HEAD_DIM),
            whole(rows, width),
        ],
        out_shape=[
            jax.ShapeDtypeStruct((shards, local, 2 * HEAD_DIM, width), BF16),
            jax.ShapeDtypeStruct((shards, 2, local, HEAD_DIM, width), BF16),
            jax.ShapeDtypeStruct((shards, local, 1, 2 * HEAD_DIM), F32),
            jax.ShapeDtypeStruct((shards, local, 1, HEAD_DIM), F32),
            jax.ShapeDtypeStruct((rows, width), F32),
        ],
        scratch_shapes=[pltpu.VMEM((rows, 2 * HEAD_DIM), BF16), pltpu.VMEM((rows, HEAD_DIM), BF16)],
    )(attn_in, grad_rows, w_qk, w_vo, qk, v, attn_out, key_bias)


def layer_stats(values):
    centred = values - jnp.mean(values, axis=-1, keepdims=True)
    inv_std = lax.rsqrt(jnp.mean(centred * centred, axis=-1, keepdims=True) + 1e-06)
    return (centred * inv_std, inv_std)


def layer_back(grad_norm, normed, inv_std):
    mean_grad = jnp.mean(grad_norm, axis=-1, keepdims=True)
    mean_proj = jnp.mean(grad_norm * normed, axis=-1, keepdims=True)
    return inv_std * (grad_norm - mean_grad - normed * mean_proj)


def gelu_both(values):
    coef = (2.0 / jnp.pi) ** 0.5
    square = values * values
    tanh = jnp.tanh(coef * values * (1.0 + 0.044715 * square))
    act = 0.5 * values * (1.0 + tanh)
    slope = 0.5 * (1.0 + tanh) + 0.5 * values * (1.0 - tanh * tanh) * coef * (
        1.0 + 3 * 0.044715 * square
    )
    return act, slope


def shift_grp(x, shift, count):
    return lax.ppermute(x, "grp", [((g + shift) % count, g) for g in range(count)])


def body(
    tokens, cond, keep_counts, orders, ada_weight, ada_bias, qkv_weight, qv_bias,
    out_weight, out_bias, fc1_weight, fc1_bias, fc2_weight, fc2_bias, cotangent,
):
    tp_rank = lax.axis_index("tp")
    grp_rank = lax.axis_index("grp")
    tp_count = lax.axis_size("tp")
    grp_count = lax.axis_size("grp")
    img_dev, tok_count, width = tokens.shape
    img_group = cond.shape[0]
    part = width // tp_count
    hidden = fc1_bias.shape[0]
    local = part // HEAD_DIM
    cap = 3 * tok_count // 4
    row_count = img_dev * cap

    split = grp_count == 4 and local % 2 == 0
    own_b = local // 2 if split else local
    rows_b = hidden * 4 // 9
    rows_x = hidden - rows_b
    if split:
        rows_b, rows_x = rows_b // 2, rows_x // 4
    way = lambda outer, low: Way(tp_count, grp_count, split, split and outer, [low])
    head_ways = [way(True, own_b * HEAD_DIM // 32 * 16), way(False, own_b * 5 * HEAD_DIM // 72 * 16)]
    ff_ways = [way(True, rows_x // 32 * 16), way(False, rows_b * 5 // 128 * 16)]
    share_x = grp_rank if split else 0
    share_b = grp_rank % 2 if split else 0
    pick = lambda x, share: lax.dynamic_index_in_dim(x, share, 0, keepdims=False)

    qkv_rows = qkv_weight.reshape(width, 3, part)
    vo = jnp.stack([qkv_rows[:, 2].T, out_weight]).reshape(-1, 2 * part // head_ways[0].shares, width)
    qk = qkv_rows[:, :2].reshape(width, 2, local, HEAD_DIM).transpose(2, 1, 3, 0)
    qk = qk.reshape(head_ways[1].shares, -1, width)
    ff_x = rows_x * ff_ways[0].shares
    pieces = [[pick(vo, share_x)], [pick(qk, share_b)]]
    for weight in (fc1_weight.T, fc2_weight):
        pieces.append([pick(weight[:ff_x].reshape(-1, rows_x, width), share_x)])
        pieces.append([pick(weight[ff_x:].reshape(-1, rows_b, width), share_b)])
    if split:
        gathered = gather_weights(
            head_ways + ff_ways + ff_ways, [2, 2, 2], pieces, tp_count, grp_count, 0
        )
    else:
        gathered = [lax.all_gather(x[None], "tp") for p in pieces for x in p]
    w_vo, w_qk, w1x, w1b, w2x, w2b = gathered
    w_vo = w_vo.reshape(tp_count, 2, local, HEAD_DIM, width)
    w_qk = w_qk.reshape(tp_count, local, 2 * HEAD_DIM, width)
    flat = lambda x: x.reshape(-1, width)

    own_orders = lax.dynamic_slice_in_dim(orders, tp_rank * img_dev, img_dev, 0)[:, :cap]
    own_counts = lax.dynamic_slice_in_dim(keep_counts, tp_rank * img_dev, img_dev, 0)
    slot = lax.broadcasted_iota(jnp.int32, (img_dev, cap), 1)
    kept = slot < own_counts[:, None]
    place_ids = lax.broadcasted_iota(jnp.int32, (1, 1, tok_count), 2)
    chosen = ((own_orders[:, :, None] == place_ids) & kept[:, :, None]).astype(BF16)
    take = lambda x: jnp.einsum("ijt,itd->ijd", chosen, x, preferred_element_type=F32)
    put = lambda x: jnp.einsum("ijt,ijd->itd", chosen, x.astype(BF16), preferred_element_type=F32)
    key_bias = jnp.where(kept, 0.0, -1e30).astype(F32)[:, None, :]
    keep_col = kept.astype(F32)[:, :, None]

    silu_cond = jax.nn.silu(cond.astype(F32)).astype(BF16)
    ada_cols = (
        jnp.einsum("id,dke->ike", silu_cond, ada_weight, preferred_element_type=F32)
        + ada_bias.astype(F32)[None]
    )
    biases = jnp.concatenate([fc1_bias, qv_bias.reshape(-1)]).astype(F32)
    mod_len = img_dev * 6 * part
    message = jnp.concatenate(
        [
            ada_cols.reshape(tp_count, mod_len),
            jnp.broadcast_to(biases[None], (tp_count, biases.shape[0])),
        ],
        axis=1,
    )
    message = lax.all_to_all(message, "tp", split_axis=0, concat_axis=0, tiled=True)
    modulation = message[:, :mod_len].reshape(tp_count, img_dev, 6, part)
    modulation = modulation.transpose(1, 2, 0, 3).reshape(img_dev, 6, width)
    shift_one, scale_one, gate_one, shift_two, scale_two, gate_two = (
        modulation[:, j][:, None, :] for j in range(6)
    )
    b1 = message[:, mod_len : mod_len + hidden]
    b1x, b1b = b1[:, :ff_x].reshape(-1, 1), b1[:, ff_x:].reshape(-1, 1)
    qv = message[:, mod_len + hidden :].reshape(tp_count, 2, local, 1, HEAD_DIM)
    qk_bias = jnp.concatenate([qv[:, 0], jnp.zeros_like(qv[:, 0])], axis=-1)
    v_bias = qv[:, 1]

    resid = take(tokens)
    grad_out = take(cotangent)
    normed_one, inv_one = layer_stats(resid)
    attn_in = (normed_one * (1.0 + scale_one) + shift_one).astype(BF16).reshape(row_count, width)
    qk, v, attn_out, branch_one = attend(attn_in, w_qk, w_vo, qk_bias, v_bias, key_bias)
    branch_one = branch_one.reshape(img_dev, cap, width) + out_bias.astype(F32)
    delta_one = keep_col * gate_one * branch_one
    hidden_res = resid + delta_one
    normed_two, inv_two = layer_stats(hidden_res)
    mlp_in = (normed_two * (1.0 + scale_two) + shift_two).astype(BF16).reshape(row_count, width)
    grad_two = (grad_out * gate_two).astype(BF16).reshape(row_count, width)
    halves = [(w1x, w2x, b1x), (w1b, w2b, b1b)]
    acts, slopes = [], []
    for w1, _, bias in halves:
        act, slope = gelu_both(dot(flat(w1), mlp_in, NT) + bias)
        acts.append(act.astype(BF16))
        slopes.append(slope.astype(BF16))
    branch_two = sum(dot(act, flat(w2), TN) for act, (_, w2, _) in zip(acts, halves))
    branch_two = branch_two.reshape(img_dev, cap, width) + fc2_bias.astype(F32)
    delta_two = keep_col * gate_two * branch_two
    block_out = tokens.astype(F32) + put(delta_one + delta_two)
    gate_grad_two = jnp.sum(grad_out * branch_two, axis=1)

    ff_parts, grads_pre = [], []
    for act, slope, (w1, w2, _) in zip(acts, slopes, halves):
        grad_pre = (dot(flat(w2), grad_two, NT) * slope.astype(F32)).astype(BF16)
        grads_pre.append(grad_pre)
        ff_parts.append(dot(act, grad_two, NN).astype(BF16).reshape(w2.shape))
    for grad_pre, (w1, _, _) in zip(grads_pre, halves):
        ff_parts.append(dot(grad_pre, mlp_in, NN).astype(BF16).reshape(w1.shape))
    fc1b_part = jnp.concatenate(
        [jnp.sum(g.astype(F32), axis=1).reshape(tp_count, -1) for g in grads_pre], axis=1
    )
    fc2b_part = jnp.sum(grad_two.astype(F32), axis=0)
    grad_mlp_in = sum(dot(g, flat(w1), TN) for g, (w1, _, _) in zip(grads_pre, halves))
    grad_mlp_in = grad_mlp_in.reshape(img_dev, cap, width)
    shift_grad_two = jnp.sum(grad_mlp_in, axis=1)
    scale_grad_two = jnp.sum(grad_mlp_in * normed_two, axis=1)
    back_two = layer_back(grad_mlp_in * (1.0 + scale_two), normed_two, inv_two)
    grad_hidden = grad_out + back_two
    gate_grad_one = jnp.sum(grad_hidden * keep_col * branch_one, axis=1)
    grad_one = (grad_hidden * keep_col * gate_one).astype(BF16).reshape(row_count, width)
    outb_part = jnp.sum(grad_one.astype(F32), axis=0)
    dqk, dvo, dqk_bias, dv_bias, grad_attn_in = attend_back(
        attn_in, grad_one, w_qk, w_vo, qk, v, attn_out, key_bias
    )
    head_parts = [
        dvo.reshape(tp_count, head_ways[0].shares, -1, width),
        dqk.reshape(tp_count, head_ways[1].shares, -1, width),
    ]
    if split:
        ff_sums = reduce_weights(ff_ways + ff_ways, ff_parts, tp_count, grp_count, 1)
        head_sums = reduce_weights(head_ways, head_parts, tp_count, grp_count, 2)
    else:
        scatter = lambda x: lax.psum_scatter(x, "tp", scatter_dimension=0)
        ff_sums, head_sums = (
            [lax.psum(scatter(x), "grp").astype(F32) for x in parts]
            for parts in (ff_parts, head_parts)
        )
    fc2_sum = jnp.concatenate([flat(ff_sums[0]), flat(ff_sums[1])])
    fc1_sum = jnp.concatenate([flat(ff_sums[2]), flat(ff_sums[3])])
    v_sum, out_sum = flat(head_sums[0])[:part], flat(head_sums[0])[part:]
    qk_sum = head_sums[1].reshape(local, 2, HEAD_DIM, width).transpose(1, 0, 2, 3)
    qkv_sum = jnp.concatenate([qk_sum.reshape(2, part, width), v_sum[None]]).transpose(2, 0, 1)

    grad_attn_in = grad_attn_in.reshape(img_dev, cap, width)
    shift_grad_one = jnp.sum(grad_attn_in, axis=1)
    scale_grad_one = jnp.sum(grad_attn_in * normed_one, axis=1)
    back_one = layer_back(grad_attn_in * (1.0 + scale_one), normed_one, inv_one)
    grad_tokens = cotangent.astype(F32) + put(back_two + back_one)

    modulation_grad = jnp.stack(
        [
            shift_grad_one, scale_grad_one, gate_grad_one,
            shift_grad_two, scale_grad_two, gate_grad_two,
        ],
        axis=1,
    )
    mod_rows = modulation_grad.reshape(img_dev, 6, tp_count, part).transpose(2, 0, 1, 3)
    message = jnp.concatenate(
        [
            mod_rows.reshape(tp_count, mod_len),
            fc1b_part,
            dqk_bias[..., :HEAD_DIM].reshape(tp_count, part),
            dv_bias.reshape(tp_count, part),
            outb_part.reshape(tp_count, part),
            fc2b_part.reshape(tp_count, part),
        ],
        axis=1,
    )
    message = lax.all_to_all(message, "tp", split_axis=0, concat_axis=0, tiled=True)
    grad_cols = message[:, :mod_len].reshape(img_group, 6, part).astype(BF16)
    bias_sums = jnp.sum(message[:, mod_len:], axis=0)
    shifts = range(1, grp_count)
    around = lambda x: [x] + [shift_grp(x, k, grp_count) for k in shifts]
    cols_all = jnp.concatenate(around(grad_cols), 0)
    silu_all = jnp.concatenate(around(silu_cond), 0)
    bias_sums = sum(around(bias_sums))
    kept_int = jnp.sum(sum(around(keep_counts)))
    kept_total = kept_int.astype(F32)
    ada_sum = jnp.einsum("id,ike->dke", silu_all, cols_all, preferred_element_type=F32)
    adab_sum = jnp.sum(cols_all.astype(F32), axis=0)
    cond_part = jnp.einsum("ike,dke->id", grad_cols, ada_weight, preferred_element_type=F32)
    cond_part = cond_part.astype(BF16).reshape(img_group, tp_count, part).transpose(1, 0, 2)
    cond_rows = lax.all_to_all(
        cond_part.reshape(tp_count, img_group * part), "tp", split_axis=0, concat_axis=0, tiled=True
    )
    cond_sum = jnp.sum(cond_rows.astype(F32), axis=0).reshape(img_group, part)
    cond_cols = lax.dynamic_slice_in_dim(cond, tp_rank * part, part, 1).astype(F32)
    cond_grad = jax.vjp(jax.nn.silu, cond_cols)[1](cond_sum)[0]

    all_tokens = img_group * tok_count * grp_count
    token_counts = jnp.stack([kept_int, all_tokens - kept_int]).astype(jnp.int32)
    at = [0, hidden, hidden + 2 * part, hidden + 3 * part, hidden + 4 * part]
    fc1b_sum, qvb_sum, outb_sum, fc2b_sum = (bias_sums[a:b] for a, b in zip(at, at[1:]))
    scaled = lambda x: x.astype(F32) / kept_total
    return (
        block_out,
        grad_tokens,
        cond_grad,
        scaled(ada_sum),
        scaled(adab_sum),
        scaled(qkv_sum),
        scaled(qvb_sum.reshape(2, part)),
        scaled(out_sum),
        scaled(outb_sum),
        scaled(fc1_sum.T),
        scaled(fc1b_sum),
        scaled(fc2_sum),
        scaled(fc2b_sum),
        token_counts,
    )


def solution(mesh):
    in_specs = (
        P(("grp", "tp"), None, None),
        P("grp", None),
        P("grp"),
        P("grp", None),
        P(None, None, "tp"),
        P(None, "tp"),
        P(None, None, "tp"),
        P(None, "tp"),
        P("tp", None),
        P(),
        P(None, "tp"),
        P("tp"),
        P("tp", None),
        P(),
        P(("grp", "tp"), None, None),
    )
    out_specs = (
        P(("grp", "tp"), None, None),
        P(("grp", "tp"), None, None),
        P("grp", "tp"),
        P(None, None, "tp"),
        P(None, "tp"),
        P(None, None, "tp"),
        P(None, "tp"),
        P("tp", None),
        P("tp"),
        P(None, "tp"),
        P("tp"),
        P("tp", None),
        P("tp"),
        P(),
    )
    return jax.shard_map(body, mesh=mesh, in_specs=in_specs, out_specs=out_specs, check_vma=False)
```
